32 devices in a mesh: gx: 4 (over z), gy: 4 (over x, core), gz: 2 (over y).
Axes of the slice: x: 2, y: 2, z: 4, core: 2. Of those that a mesh axis runs over, the one named last changes fastest.
Arguments:
- phase: int32 [4, 8, 64], P('gx', 'gy', 'gz'), may hold values from 0 to 1
- lame: float32 [2, 2], replicated, may hold values from 0.3 to 10
- start: float32 [3, 32, 16, 32, 256], P(None, None, 'gx', 'gy', 'gz'), may hold values from -6 to 6
Outputs:
- basis: float32 [3, 32, 16, 32, 256], P(None, None, 'gx', 'gy', 'gz')
- coarse: float32 [32, 32], replicated
The draws below stay inside these ranges and needn't reach their ends.
All inputs are finite; a program needn't handle non-finite values.
Results may differ from the reference program's by a relative error of at most 0.0001.
Values sent between devices are 32-bit elements; how exact they have to be, the bound alone decides.
A program may use at most 64 MiB of HBM per device.

```python
import math
import jax
import jax.numpy as jnp
from jax import lax

VECS = 32
ITERS = 3
PHASES = 2
BRICK = 4
NX = 16
NY = 32
NZ = 256


def touch_ends(array, rng, low, high):
    place = [jax.random.randint(jax.random.fold_in(rng, axis), (), 0, length) for axis, length in enumerate(array.shape)]
    widest = array.shape.index(max(array.shape))
    next_to = place[:widest] + [(place[widest] + 1) % array.shape[widest]] + place[widest + 1:]
    return array.at[tuple(place)].set(low).at[tuple(next_to)].set(high)


def steps_of(own_key, dims, pieces, low, top_value):
    def one(axis_at, blocks):
        draws = jax.random.uniform(jax.random.fold_in(jax.random.fold_in(own_key, 6), axis_at), (blocks,), jnp.float32, low / len(pieces), top_value / len(pieces))
        return jnp.repeat(jnp.exp(draws), dims[axis_at] // blocks).reshape((-1,) + (1,) * (len(dims) - axis_at - 1))

    gain = one(*pieces[0])
    for cut in pieces[1:]:
        gain = gain * one(*cut)
    return gain


def normal_values(key, shape, spread, reach, split=(), kind=jnp.bfloat16):
    values = jax.random.normal(key, shape, jnp.float32) * spread
    if len(split) > 0:
        values = steps_of(key, shape, split, -0.22, 0.18) * values
    return jnp.clip(values, min=-reach, max=reach).astype(kind)


def setup_inputs(seed: int = 0) -> dict:
    key_list = jax.random.split(jax.random.key(seed), 4)
    phase = touch_ends(jax.random.randint(key_list[0], (NX // BRICK, NY // BRICK, NZ // BRICK), 0, PHASES), jax.random.fold_in(key_list[0], 1), 0, PHASES - 1).astype(jnp.int32)
    lame = jnp.clip(jnp.exp(jax.random.uniform(key_list[1], (PHASES, 2), jnp.float32, math.log(0.3), math.log(10.0))), 0.3, 10.0)
    start = normal_values(key_list[2], (3, VECS, NX, NY, NZ), 1.0, 6.0, ((2, 4), (3, 4), (4, 2)), jnp.float32)
    return dict(phase=phase, lame=lame, start=start)


def node_fields(padded_bricks, lame):
    nodes = jnp.repeat(jnp.repeat(jnp.repeat(padded_bricks, BRICK, 0), BRICK, 1), BRICK, 2)
    cut = BRICK - 1
    nodes = nodes[cut:-cut, cut:-cut, cut:-cut]
    shear = jnp.zeros(nodes.shape, jnp.float32)
    first = jnp.zeros(nodes.shape, jnp.float32)
    for index in range(PHASES):
        hit = nodes == index
        shear = shear + jnp.where(hit, lame[index, 0], 0.0)
        first = first + jnp.where(hit, lame[index, 1], 0.0)
    return (shear, first + shear)

def stencil(padded, shear, grow):
    centre = padded[:, :, 1:-1, 1:-1, 1:-1]
    shear_c = shear[1:-1, 1:-1, 1:-1]
    grow_c = grow[1:-1, 1:-1, 1:-1]
    total = jnp.zeros(centre.shape, centre.dtype)
    for axis_d in range(3):
        length = centre.shape[2 + axis_d]
        for offset in (0, 2):
            cuts = [slice(1, -1), slice(1, -1), slice(1, -1)]
            cuts[axis_d] = slice(offset, offset + length)
            cuts = tuple(cuts)
            beside = padded[(slice(None), slice(None)) + cuts]
            w_shear = 0.5 * (shear_c + shear[cuts])
            w_grow = 0.5 * (grow_c + grow[cuts])
            weight = jnp.stack([w_shear + w_grow if comp == axis_d else w_shear for comp in range(3)])
            total = total + weight[:, None] * (centre - beside)
    return total

def inner(left, right):
    return jnp.einsum('ckxyz,clxyz->kl', left, right, precision=lax.Precision.HIGHEST)

def inverse_factor(gram):
    lower_f = jnp.linalg.cholesky(gram)
    return lax.linalg.triangular_solve(lower_f, jnp.eye(gram.shape[0], dtype=jnp.float32), left_side=True, lower=True)

def reference(phase, lame, start):
    total_rows = 3.0 * start.shape[2] * start.shape[3] * start.shape[4]
    shear, grow = node_fields(jnp.pad(phase, 1), lame)
    widths = ((0, 0), (0, 0), (1, 1), (1, 1), (1, 1))
    block = start
    for step in range(ITERS):
        image = stencil(jnp.pad(block, widths), shear, grow)
        factor = inverse_factor(inner(image, image) / total_rows)
        block = jnp.einsum('kl,clxyz->ckxyz', factor, image, precision=lax.Precision.HIGHEST)
    applied = stencil(jnp.pad(block, widths), shear, grow)
    return (block, inner(block, applied) / total_rows)
```

```python
import functools

import jax
import jax.numpy as jnp
from jax import lax
from jax.experimental import pallas as pl
from jax.experimental.pallas import tpu as pltpu
from jax.sharding import PartitionSpec as P

ITERS = 3
PHASES = 2
BRICK = 4
PIECES = 3
UNROLL = 2
AXES = ("gx", "gy", "gz")
MESH = pl.DeviceIdType.MESH
F32 = jnp.float32
BF16 = jnp.bfloat16


def split(value):
    pieces = []
    for _ in range(PIECES):
        piece = value.astype(BF16)
        pieces.append(piece)
        value = value - piece.astype(F32)
    return jnp.concatenate(pieces, axis=0)


def contract_last(left, right):
    return lax.dot_general(
        left, right, (((1,), (1,)), ((), ())), preferred_element_type=F32
    )


def exact_dot(left, right):
    return jnp.dot(
        left, right, precision=lax.Precision.HIGHEST, preferred_element_type=F32
    )


def fold(blocks, size):
    rows = blocks[:size]
    for k in range(1, PIECES):
        rows = rows + blocks[k * size : (k + 1) * size]
    total = rows[:, :size]
    for k in range(1, PIECES):
        total = total + rows[:, k * size : (k + 1) * size]
    return total


def inverse_factor(gram, size):
    row = lax.broadcasted_iota(jnp.int32, (size, size), 0)
    col = lax.broadcasted_iota(jnp.int32, (size, size), 1)
    both = jnp.concatenate([gram, jnp.where(row == col, 1.0, 0.0).astype(F32)], axis=1)
    rows = lax.broadcasted_iota(jnp.int32, both.shape, 0)
    for j in range(size):
        scale = lax.rsqrt(both[j : j + 1, j : j + 1])
        pivot = both[j : j + 1, :] * scale
        column = both[:, j : j + 1] * scale
        both = jnp.where(
            rows > j, both - column * pivot, jnp.where(rows == j, pivot, both)
        )
    return both[:, size:]


def kernel(
    counts,
    dims,
    lame,
    phase,
    start,
    basis,
    coarse,
    field,
    stage,
    edge_out,
    edge_in,
    edge_now,
    phase_own,
    phase_in,
    weights,
    parts,
    image_parts,
    sums,
    local_sem,
    phase_send,
    phase_recv,
    send_sem,
    recv_sem,
    sum_send,
    sum_recv,
):
    parts_c, vecs, nx, ny, nz = dims
    nodes = nx * ny
    total_rows = 1.0 * parts_c * nodes * nz * counts[0] * counts[1] * counts[2]
    me = [lax.axis_index(axis) for axis in AXES]
    half = ny // 2

    loads = [
        pltpu.make_async_copy(start.at[c], stage.at[c], local_sem.at[c])
        for c in range(parts_c)
    ]
    for copy in loads:
        copy.start()

    def has(side):
        axis = side // 2
        return me[axis] > 0 if side % 2 == 0 else me[axis] < counts[axis] - 1

    def lacks(side):
        axis = side // 2
        return me[axis] == 0 if side % 2 == 0 else me[axis] == counts[axis] - 1

    def beside(side):
        axis = side // 2
        return {AXES[axis]: me[axis] - 1 if side % 2 == 0 else me[axis] + 1}

    plane = jnp.zeros((vecs, nz), F32)
    for side in range(2):
        at = 0 if side == 0 else nx + 1

        @pl.when(lacks(side))
        def _(at=at):
            def clear(i, _):
                for s in range(ITERS + 1):
                    for c in range(parts_c):
                        field[s, c, at, i + 1] = plane
                return 0

            lax.fori_loop(0, ny, clear, 0)

    for side in range(2, 4):
        at = 0 if side == 2 else ny + 1

        @pl.when(lacks(side))
        def _(at=at):
            def clear(i, _):
                for s in range(ITERS + 1):
                    for c in range(parts_c):
                        field[s, c, i + 1, at] = plane
                return 0

            lax.fori_loop(0, nx, clear, 0)

    def clear_half(i, _):
        for c in range(parts_c):
            field[ITERS, c, 0, half + i + 1] = plane
            field[ITERS, c, nx + 1, i + 1] = plane
        return 0

    lax.fori_loop(0, half, clear_half, 0)
    edge_in[...] = jnp.zeros(edge_in.shape, F32)
    phase_in[...] = jnp.zeros(phase_in.shape, F32)

    bricks_x, bricks_y, bricks_z = phase.shape
    spread = jnp.where(
        lax.broadcasted_iota(jnp.int32, (bricks_z, nz), 1) // BRICK
        == lax.broadcasted_iota(jnp.int32, (bricks_z, nz), 0),
        1.0,
        0.0,
    ).astype(F32)
    row_brick = lax.broadcasted_iota(jnp.int32, (ny, bricks_z), 0) // BRICK
    for bx in range(bricks_x):
        own = phase[bx].astype(F32)
        rows = jnp.zeros((ny, bricks_z), F32)
        for by in range(bricks_y):
            rows = jnp.where(
                row_brick == by,
                jnp.broadcast_to(own[by : by + 1], (ny, bricks_z)),
                rows,
            )
        phase_own[bx] = jnp.dot(rows, spread, preferred_element_type=F32)

    barrier = pltpu.get_barrier_semaphore()
    for axis in range(3):
        for k in range(counts[axis]):

            @pl.when(me[axis] != k)
            def _(axis=axis, k=k):
                pl.semaphore_signal(
                    barrier, inc=1, device_id={AXES[axis]: k}, device_id_type=MESH
                )

    def face(s, c, side):
        if side == 0:
            src, dst = field.at[s, c, 1], field.at[s, c, nx + 1]
        elif side == 1:
            src, dst = field.at[s, c, nx], field.at[s, c, 0]
        elif side == 2:
            src = field.at[s, c, pl.ds(1, nx), 1]
            dst = field.at[s, c, pl.ds(1, nx), ny + 1]
        elif side == 3:
            src = field.at[s, c, pl.ds(1, nx), ny]
            dst = field.at[s, c, pl.ds(1, nx), 0]
        else:
            src, dst = edge_out.at[s, c], edge_in.at[s, c, 1 - side % 2]
        if side < 2:
            if s < ITERS:
                rows = pl.ds(1, ny)
            elif side == 0:
                rows = pl.ds(half + 1, ny - half)
            else:
                rows = pl.ds(1, half)
            src, dst = src.at[rows], dst.at[rows]
        return src, dst

    def send_copy(s, c, side):
        src, dst = face(s, c, side)
        return pltpu.make_async_remote_copy(
            src_ref=src,
            dst_ref=dst,
            send_sem=send_sem.at[s, c, side],
            recv_sem=recv_sem.at[s, c, side ^ 1],
            device_id=beside(side),
            device_id_type=MESH,
        )

    def recv_copy(s, c, side):
        src, dst = face(s, c, side ^ 1)
        return pltpu.make_async_remote_copy(
            src_ref=src,
            dst_ref=dst,
            send_sem=send_sem.at[s, c, side],
            recv_sem=recv_sem.at[s, c, side],
            device_id=beside(side),
            device_id_type=MESH,
        )

    def each_side(action):
        for side in range(6):

            @pl.when(has(side))
            def _(side=side):
                action(side)

    def send(s, c):
        each_side(lambda side: send_copy(s, c, side).start())

    def receive(s, c):
        each_side(lambda side: recv_copy(s, c, side).wait_recv())

    def phase_copy(side, signal):
        return pltpu.make_async_remote_copy(
            src_ref=phase_own,
            dst_ref=phase_in.at[signal],
            send_sem=phase_send.at[side],
            recv_sem=phase_recv.at[signal],
            device_id=beside(side),
            device_id_type=MESH,
        )

    lane = lax.broadcasted_iota(jnp.int32, (vecs, nz), 1)
    empty = jnp.zeros((vecs, nz), F32)

    def take_edges(edges, value, i):
        here = lax.rem(lane + (nz + 1 - 2 * i), nz) < 2
        return jnp.where(here, pltpu.roll(value, 2 * i, 1), edges)

    for c in range(parts_c):
        loads[c].wait()

        def bring(k, edges, c=c):
            for t in range(UNROLL):
                i = k * UNROLL + t
                value = stage[c, pl.ds(i, vecs, stride=nodes), :]
                field[0, c, i // ny + 1, lax.rem(i, ny) + 1] = value
                edges = take_edges(edges, value, i)
            return edges

        edge_out[0, c] = lax.fori_loop(0, nodes // UNROLL, bring, empty)
        if c == 0:
            pl.semaphore_wait(barrier, sum(counts) - 3)
            each_side(lambda side: phase_copy(side, side ^ 1).start())
        send(0, c)

    each_side(lambda side: phase_copy(side, side).wait_recv())
    line = lax.broadcasted_iota(jnp.int32, (ny, nz), 0)
    across = lax.broadcasted_iota(jnp.int32, (ny, nz), 1)

    def material(kinds):
        shear = jnp.zeros(kinds.shape, F32)
        first = jnp.zeros(kinds.shape, F32)
        for index in range(PHASES):
            hit = kinds == float(index)
            shear = shear + jnp.where(hit, lame[index, 0], 0.0)
            first = first + jnp.where(hit, lame[index, 1], 0.0)
        return shear, first + shear

    for x in range(nx):
        bx = x // BRICK
        own = phase_own[bx]
        others = [
            phase_own[(x - 1) // BRICK] if x > 0 else phase_in[0, bricks_x - 1],
            phase_own[(x + 1) // BRICK] if x < nx - 1 else phase_in[1, 0],
            pltpu.roll(jnp.where(line == ny - 1, phase_in[2, bx], own), 1, 0),
            pltpu.roll(jnp.where(line == 0, phase_in[3, bx], own), ny - 1, 0),
            pltpu.roll(jnp.where(across == nz - 1, phase_in[4, bx], own), 1, 1),
            pltpu.roll(jnp.where(across == 0, phase_in[5, bx], own), nz - 1, 1),
        ]
        shear_c, grow_c = material(own)
        for side in range(6):
            shear_n, grow_n = material(others[side])
            w_shear = 0.5 * (shear_c + shear_n)
            w_grow = 0.5 * (grow_c + grow_n)
            weights[2 * side, pl.ds(x * ny, ny), :] = w_shear
            weights[2 * side + 1, pl.ds(x * ny, ny), :] = w_shear + w_grow

    def image(s, c, i):
        x, y = i // ny, lax.rem(i, ny)
        centre = field[s, c, x + 1, y + 1]
        border = pltpu.roll(edge_now[...], lax.rem(2 * nz - 2 * i, nz), 1)
        others = [
            field[s, c, x, y + 1],
            field[s, c, x + 2, y + 1],
            field[s, c, x + 1, y],
            field[s, c, x + 1, y + 2],
            pltpu.roll(jnp.where(lane == nz - 1, border, centre), 1, 1),
            pltpu.roll(jnp.where(lane == 0, border, centre), nz - 1, 1),
        ]
        total = None
        for side in range(6):
            which = 2 * side + (1 if side // 2 == c else 0)
            weight = weights[which, pl.ds(i, 1), :]
            term = weight * (centre - others[side])
            total = term if total is None else total + term
        return total

    def ready(s, c):
        receive(s, c)
        edge_now[...] = jnp.where(
            lax.rem(lane, 2) == 0, edge_in[s, c, 1], edge_in[s, c, 0]
        )

    def product(c, other):
        def body(x, total):
            left = jnp.concatenate(
                [parts[c, x * ny + y] for y in range(ny)], axis=1
            )
            right = (
                left
                if other is None
                else jnp.concatenate([other[x * ny + y] for y in range(ny)], axis=1)
            )
            return total + contract_last(left, right)

        size = PIECES * vecs
        return lax.fori_loop(0, nx, body, jnp.zeros((size, size), F32))

    offsets = [0, counts[0], counts[0] + counts[1]]

    def sum_copy(which, axis, slot, other):
        at = offsets[axis] + slot
        return pltpu.make_async_remote_copy(
            src_ref=sums.at[which, at],
            dst_ref=sums.at[which, at],
            send_sem=sum_send.at[which, offsets[axis] + other],
            recv_sem=sum_recv.at[which, at],
            device_id={AXES[axis]: other},
            device_id_type=MESH,
        )

    def sum_start(which, axis, value):
        sums[which, offsets[axis] + me[axis]] = value
        for k in range(counts[axis]):

            @pl.when(me[axis] != k)
            def _(k=k):
                sum_copy(which, axis, me[axis], k).start()

    def sum_end(which, axis):
        for k in range(counts[axis]):

            @pl.when(me[axis] != k)
            def _(k=k):
                sum_copy(which, axis, k, k).wait_recv()

        total = sums[which, offsets[axis]]
        for k in range(1, counts[axis]):
            total = total + sums[which, offsets[axis] + k]
        return total

    def padded(square):
        return jnp.concatenate([square, jnp.zeros((vecs, nz - vecs), F32)], axis=1)

    gram = None
    for s in range(ITERS):
        last = s == ITERS - 1
        for c in range(parts_c):
            ready(s, c)

            def step(k, edges, s=s, c=c, last=last):
                for t in range(UNROLL):
                    i = k * UNROLL + t
                    value = image(s, c, i)
                    field[s + 1, c, i // ny + 1, lax.rem(i, ny) + 1] = value
                    edges = take_edges(edges, value, i)
                    if last:
                        parts[c, i] = split(value)
                return edges

            edge_out[s + 1, c] = lax.fori_loop(0, nodes // UNROLL, step, empty)
            send(s + 1, c)
            if last:
                more = product(c, None)
                gram = more if gram is None else gram + more

    sum_start(0, 0, padded(fold(gram, vecs)))

    cross = None
    value = None
    for c in range(parts_c):
        ready(ITERS, c)

        def twice(y, _, c=c):
            low = field[ITERS, c, 0, y + 1]
            high = field[ITERS, c, nx + 1, half + y + 1]
            field[ITERS, c, 0, y + 1] = low + low
            field[ITERS, c, nx + 1, half + y + 1] = high + high
            return 0

        lax.fori_loop(0, half, twice, 0)

        def last_step(k, _, c=c):
            for t in range(UNROLL):
                i = k * UNROLL + t
                image_parts[i] = split(image(ITERS, c, i))
            return 0

        lax.fori_loop(0, nodes // UNROLL, last_step, 0)
        more = product(c, image_parts)
        cross = more if cross is None else cross + more
        value = sum_end(0, c)
        if c < 2:
            sum_start(0, c + 1, value)

    sum_start(1, 0, padded(fold(cross, vecs)))
    mixing = inverse_factor(value[:, :vecs] / total_rows, vecs)
    pieces = split(mixing)
    high, middle, low = (pieces[k * vecs : (k + 1) * vecs] for k in range(PIECES))
    none = jnp.zeros((vecs, vecs), BF16)
    mixer = jnp.concatenate(
        [
            jnp.concatenate([high, high, high], axis=1),
            jnp.concatenate([middle, middle, none], axis=1),
            jnp.concatenate([low, none, none], axis=1),
        ],
        axis=0,
    )

    stores = []
    for c in range(parts_c):

        def mix(k, _, c=c):
            for t in range(UNROLL):
                i = k * UNROLL + t
                out = jnp.dot(mixer, parts[c, i], preferred_element_type=F32)
                stage[c, pl.ds(i, vecs, stride=nodes), :] = (
                    out[:vecs] + out[vecs : 2 * vecs] + out[2 * vecs :]
                )
            return 0

        lax.fori_loop(0, nodes // UNROLL, mix, 0)
        copy = pltpu.make_async_copy(stage.at[c], basis.at[c], local_sem.at[c])
        copy.start()
        stores.append(copy)
        value = sum_end(1, c)
        if c < 2:
            sum_start(1, c + 1, value)

    form = value[:, :vecs]
    form = 0.5 * (form + form.T)
    first = exact_dot(mixing, form)
    coarse[...] = (
        lax.dot_general(
            first,
            mixing,
            (((1,), (1,)), ((), ())),
            precision=lax.Precision.HIGHEST,
            preferred_element_type=F32,
        )
        / total_rows
    )

    for s in range(ITERS + 1):
        for c in range(parts_c):
            each_side(lambda side: send_copy(s, c, side).wait_send())
    each_side(lambda side: phase_copy(side, side ^ 1).wait_send())
    for which in range(2):
        for axis in range(3):
            for k in range(counts[axis]):

                @pl.when(me[axis] != k)
                def _(which=which, axis=axis, k=k):
                    sum_copy(which, axis, me[axis], k).wait_send()

    for copy in stores:
        copy.wait()


def on_device(counts, phase, lame, start):
    comps, vecs, nx, ny, nz = dims = start.shape
    nodes = nx * ny
    assert comps == 3 and 2 * nodes <= nz and ny % 2 == 0
    slots = sum(counts)
    steps = ITERS + 1
    basis, coarse = pl.pallas_call(
        functools.partial(kernel, counts, dims),
        out_shape=(
            jax.ShapeDtypeStruct((comps, vecs * nodes, nz), F32),
            jax.ShapeDtypeStruct((vecs, vecs), F32),
        ),
        in_specs=[
            pl.BlockSpec(memory_space=pltpu.SMEM),
            pl.BlockSpec(memory_space=pltpu.VMEM),
            pl.BlockSpec(memory_space=pl.ANY),
        ],
        out_specs=(
            pl.BlockSpec(memory_space=pl.ANY),
            pl.BlockSpec(memory_space=pltpu.VMEM),
        ),
        scratch_shapes=[
            pltpu.VMEM((steps, comps, nx + 2, ny + 2, vecs, nz), F32),
            pltpu.VMEM((comps, vecs * nodes, nz), F32),
            pltpu.VMEM((steps, comps, vecs, nz), F32),
            pltpu.VMEM((steps, comps, 2, vecs, nz), F32),
            pltpu.VMEM((vecs, nz), F32),
            pltpu.VMEM((phase.shape[0], ny, nz), F32),
            pltpu.VMEM((6, phase.shape[0], ny, nz), F32),
            pltpu.VMEM((12, nodes, nz), F32),
            pltpu.VMEM((comps, nodes, PIECES * vecs, nz), BF16),
            pltpu.VMEM((nodes, PIECES * vecs, nz), BF16),
            pltpu.VMEM((2, slots, vecs, nz), F32),
            pltpu.SemaphoreType.DMA((comps,)),
            pltpu.SemaphoreType.DMA((6,)),
            pltpu.SemaphoreType.DMA((6,)),
            pltpu.SemaphoreType.DMA((steps, comps, 6)),
            pltpu.SemaphoreType.DMA((steps, comps, 6)),
            pltpu.SemaphoreType.DMA((2, slots)),
            pltpu.SemaphoreType.DMA((2, slots)),
        ],
        compiler_params=pltpu.CompilerParams(
            collective_id=0, has_side_effects=True, vmem_limit_bytes=48 * 1024 * 1024
        ),
    )(lame, phase, start.reshape(comps, vecs * nodes, nz))
    return basis.reshape(start.shape), coarse


def solution(mesh):
    counts = tuple(mesh.shape[axis] for axis in AXES)
    spread = P(None, None, *AXES)
    return jax.shard_map(
        functools.partial(on_device, counts),
        mesh=mesh,
        in_specs=(P(*AXES), P(), spread),
        out_specs=(spread, P()),
        check_vma=False,
    )
```

```python
import functools

import jax
import jax.numpy as jnp
from jax import lax
from jax.experimental import pallas as pl
from jax.experimental.pallas import tpu as pltpu
from jax.sharding import PartitionSpec as P

ITERS = 3
PHASES = 2
BRICK = 4
PIECES = 3
GROUP = 4
AXES = ("gx", "gy", "gz")
MESH = pl.DeviceIdType.MESH
F32 = jnp.float32
BF16 = jnp.bfloat16


def split(value):
    pieces = []
    for _ in range(PIECES):
        piece = value.astype(BF16)
        pieces.append(piece)
        value = value - piece.astype(F32)
    return jnp.concatenate(pieces, axis=0)


def contract_last(left, right):
    return lax.dot_general(
        left, right, (((1,), (1,)), ((), ())), preferred_element_type=F32
    )


def exact_dot(left, right):
    return jnp.dot(
        left, right, precision=lax.Precision.HIGHEST, preferred_element_type=F32
    )


def fold(blocks, size):
    rows = blocks[:size]
    for k in range(1, PIECES):
        rows = rows + blocks[k * size : (k + 1) * size]
    total = rows[:, :size]
    for k in range(1, PIECES):
        total = total + rows[:, k * size : (k + 1) * size]
    return total


def inverse_factor(gram, size):
    row = lax.broadcasted_iota(jnp.int32, (size, size), 0)
    col = lax.broadcasted_iota(jnp.int32, (size, size), 1)
    both = jnp.concatenate([gram, jnp.where(row == col, 1.0, 0.0).astype(F32)], axis=1)
    rows = lax.broadcasted_iota(jnp.int32, both.shape, 0)
    for j in range(size):
        scale = lax.rsqrt(both[j : j + 1, j : j + 1])
        pivot = both[j : j + 1, :] * scale
        column = both[:, j : j + 1] * scale
        both = jnp.where(
            rows > j, both - column * pivot, jnp.where(rows == j, pivot, both)
        )
    return both[:, size:]


def kernel(
    counts,
    dims,
    lame_in,
    phase_hbm,
    start,
    basis,
    coarse,
    lame,
    phase,
    field,
    stage,
    edge_out,
    edge_in,
    edge_now,
    phase_own,
    phase_in,
    weights,
    parts,
    image_parts,
    sums,
    local_sem,
    phase_send,
    phase_recv,
    send_sem,
    recv_sem,
    sum_send,
    sum_recv,
):
    parts_c, vecs, nx, ny, nz = dims
    nodes = nx * ny
    total_rows = 1.0 * parts_c * nodes * nz * counts[0] * counts[1] * counts[2]
    me = [lax.axis_index(axis) for axis in AXES]
    half = ny // 2

    small = [
        pltpu.make_async_copy(phase_hbm, phase, local_sem.at[parts_c]),
        pltpu.make_async_copy(lame_in, lame, local_sem.at[parts_c + 1]),
    ]
    for copy in small:
        copy.start()

    def place(k):
        each = ny // GROUP
        return lax.div(k, each), lax.rem(k, each) * GROUP, k * GROUP

    for c in range(parts_c):

        def fetch(k, _, c=c):
            x, y, _i = place(k)
            for t in range(GROUP):
                pltpu.make_async_copy(
                    start.at[c, :, x, y + t],
                    field.at[0, c, x + 1, y + t + 1],
                    local_sem.at[c],
                ).start()
            return 0

        lax.fori_loop(0, nodes // GROUP, fetch, 0)

    inner = (pl.ds(1, nx), pl.ds(1, ny))

    def has(side):
        axis = side // 2
        return me[axis] > 0 if side % 2 == 0 else me[axis] < counts[axis] - 1

    def lacks(side):
        axis = side // 2
        return me[axis] == 0 if side % 2 == 0 else me[axis] == counts[axis] - 1

    def beside(side):
        axis = side // 2
        return {AXES[axis]: me[axis] - 1 if side % 2 == 0 else me[axis] + 1}

    plane = jnp.zeros((vecs, nz), F32)
    for side in range(2):
        at = 0 if side == 0 else nx + 1

        @pl.when(lacks(side))
        def _(at=at):
            def clear(i, _):
                for s in range(ITERS + 1):
                    for c in range(parts_c):
                        field[s, c, at, i + 1] = plane
                return 0

            lax.fori_loop(0, ny, clear, 0)

    for side in range(2, 4):
        at = 0 if side == 2 else ny + 1

        @pl.when(lacks(side))
        def _(at=at):
            def clear(i, _):
                for s in range(ITERS + 1):
                    for c in range(parts_c):
                        field[s, c, i + 1, at] = plane
                return 0

            lax.fori_loop(0, nx, clear, 0)

    def clear_half(i, _):
        for c in range(parts_c):
            field[ITERS, c, 0, half + i + 1] = plane
            field[ITERS, c, nx + 1, i + 1] = plane
        return 0

    lax.fori_loop(0, half, clear_half, 0)
    edge_in[...] = jnp.zeros(edge_in.shape, F32)
    phase_in[...] = jnp.zeros(phase_in.shape, F32)

    for copy in small:
        copy.wait()
    bricks_x, bricks_y, bricks_z = phase.shape
    spread = jnp.where(
        lax.broadcasted_iota(jnp.int32, (bricks_z, nz), 1) // BRICK
        == lax.broadcasted_iota(jnp.int32, (bricks_z, nz), 0),
        1.0,
        0.0,
    ).astype(F32)
    row_brick = lax.broadcasted_iota(jnp.int32, (ny, bricks_z), 0) // BRICK
    for bx in range(bricks_x):
        own = phase[bx].astype(F32)
        rows = jnp.zeros((ny, bricks_z), F32)
        for by in range(bricks_y):
            rows = jnp.where(
                row_brick == by,
                jnp.broadcast_to(own[by : by + 1], (ny, bricks_z)),
                rows,
            )
        phase_own[bx] = jnp.dot(rows, spread, preferred_element_type=F32)

    barrier = pltpu.get_barrier_semaphore()
    for axis in range(3):
        for k in range(counts[axis]):

            @pl.when(me[axis] != k)
            def _(axis=axis, k=k):
                pl.semaphore_signal(
                    barrier, inc=1, device_id={AXES[axis]: k}, device_id_type=MESH
                )

    def face(s, c, side):
        if side == 0:
            src, dst = field.at[s, c, 1], field.at[s, c, nx + 1]
        elif side == 1:
            src, dst = field.at[s, c, nx], field.at[s, c, 0]
        elif side == 2:
            src = field.at[s, c, pl.ds(1, nx), 1]
            dst = field.at[s, c, pl.ds(1, nx), ny + 1]
        elif side == 3:
            src = field.at[s, c, pl.ds(1, nx), ny]
            dst = field.at[s, c, pl.ds(1, nx), 0]
        else:
            src, dst = edge_out.at[s, c], edge_in.at[s, c, 1 - side % 2]
        if side < 2:
            if s < ITERS:
                rows = pl.ds(1, ny)
            elif side == 0:
                rows = pl.ds(half + 1, ny - half)
            else:
                rows = pl.ds(1, half)
            src, dst = src.at[rows], dst.at[rows]
        return src, dst

    def send_copy(s, c, side):
        src, dst = face(s, c, side)
        return pltpu.make_async_remote_copy(
            src_ref=src,
            dst_ref=dst,
            send_sem=send_sem.at[s, c, side],
            recv_sem=recv_sem.at[s, c, side ^ 1],
            device_id=beside(side),
            device_id_type=MESH,
        )

    def recv_copy(s, c, side):
        src, dst = face(s, c, side ^ 1)
        return pltpu.make_async_remote_copy(
            src_ref=src,
            dst_ref=dst,
            send_sem=send_sem.at[s, c, side],
            recv_sem=recv_sem.at[s, c, side],
            device_id=beside(side),
            device_id_type=MESH,
        )

    lane = lax.broadcasted_iota(jnp.int32, (vecs, nz), 1)
    pair = lax.rem(lax.div(lane + 1, 2), nz // 2)

    def each_side(action, sides=range(6)):
        for side in sides:

            @pl.when(has(side))
            def _(side=side):
                action(side)

    def send(s, c):
        each_side(lambda side: send_copy(s, c, side).start(), range(4))
        edges = jnp.zeros((vecs, nz), F32)
        for i in range(nodes):
            value = field[s, c, i // ny + 1, i % ny + 1]
            edges = jnp.where(
                pair == i, pltpu.roll(value, 2 * i, 1) if i else value, edges
            )
        edge_out[s, c] = edges
        each_side(lambda side: send_copy(s, c, side).start(), range(4, 6))

    def receive(s, c):
        each_side(lambda side: recv_copy(s, c, side).wait_recv())

    def phase_copy(side, signal):
        return pltpu.make_async_remote_copy(
            src_ref=phase_own,
            dst_ref=phase_in.at[signal],
            send_sem=phase_send.at[side],
            recv_sem=phase_recv.at[signal],
            device_id=beside(side),
            device_id_type=MESH,
        )

    for c in range(parts_c):
        pltpu.make_async_copy(
            field.at[(1, c) + inner], field.at[(0, c) + inner], local_sem.at[c]
        ).wait()
        if c == 0:
            pl.semaphore_wait(barrier, sum(counts) - 3)
            each_side(lambda side: phase_copy(side, side ^ 1).start())
        send(0, c)

    each_side(lambda side: phase_copy(side, side).wait_recv())
    line = lax.broadcasted_iota(jnp.int32, (ny, nz), 0)
    across = lax.broadcasted_iota(jnp.int32, (ny, nz), 1)

    def material(kinds):
        shear = jnp.zeros(kinds.shape, F32)
        first = jnp.zeros(kinds.shape, F32)
        for index in range(PHASES):
            hit = kinds == float(index)
            shear = shear + jnp.where(hit, lame[index, 0], 0.0)
            first = first + jnp.where(hit, lame[index, 1], 0.0)
        return shear, first + shear

    for x in range(nx):
        bx = x // BRICK
        own = phase_own[bx]
        others = [
            phase_own[(x - 1) // BRICK] if x > 0 else phase_in[0, bricks_x - 1],
            phase_own[(x + 1) // BRICK] if x < nx - 1 else phase_in[1, 0],
            pltpu.roll(jnp.where(line == ny - 1, phase_in[2, bx], own), 1, 0),
            pltpu.roll(jnp.where(line == 0, phase_in[3, bx], own), ny - 1, 0),
            pltpu.roll(jnp.where(across == nz - 1, phase_in[4, bx], own), 1, 1),
            pltpu.roll(jnp.where(across == 0, phase_in[5, bx], own), nz - 1, 1),
        ]
        shear_c, grow_c = material(own)
        for side in range(6):
            shear_n, grow_n = material(others[side])
            w_shear = 0.5 * (shear_c + shear_n)
            w_grow = 0.5 * (grow_c + grow_n)
            weights[2 * side, pl.ds(x * ny, ny), :] = w_shear
            weights[2 * side + 1, pl.ds(x * ny, ny), :] = w_shear + w_grow

    def image(s, c, k):
        x, y, i = place(k)
        column = [field[s, c, x + 1, y + t] for t in range(GROUP + 2)]
        edges = edge_now[...]
        totals = []
        for t in range(GROUP):
            centre = column[t + 1]
            border = pltpu.roll(edges, nz - 2 * t - 2 * i, 1)
            others = [
                field[s, c, x, y + t + 1],
                field[s, c, x + 2, y + t + 1],
                column[t],
                column[t + 2],
                jnp.where(lane == 0, border, pltpu.roll(centre, 1, 1)),
                jnp.where(lane == nz - 1, border, pltpu.roll(centre, nz - 1, 1)),
            ]
            total = None
            for side in range(6):
                which = 2 * side + (1 if side // 2 == c else 0)
                weight = weights[which, pl.ds(i + t, 1), :]
                term = weight * (centre - others[side])
                total = term if total is None else total + term
            totals.append(total)
        return totals

    def ready(s, c):
        receive(s, c)
        edge_now[...] = jnp.where(
            lax.rem(lane, 2) == 0,
            pltpu.roll(edge_in[s, c, 0], 1, 1),
            pltpu.roll(edge_in[s, c, 1], nz - 1, 1),
        )

    def product(c, other):
        total = None
        for x in range(nx):
            left = jnp.concatenate(
                [parts[c, x * ny + y] for y in range(ny)], axis=1
            )
            right = (
                left
                if other is None
                else jnp.concatenate([other[x * ny + y] for y in range(ny)], axis=1)
            )
            more = contract_last(left, right)
            total = more if total is None else total + more
        return total

    offsets = [0, counts[0], counts[0] + counts[1]]

    def sum_copy(which, axis, slot, other):
        at = offsets[axis] + slot
        return pltpu.make_async_remote_copy(
            src_ref=sums.at[which, at],
            dst_ref=sums.at[which, at],
            send_sem=sum_send.at[which, offsets[axis] + other],
            recv_sem=sum_recv.at[which, at],
            device_id={AXES[axis]: other},
            device_id_type=MESH,
        )

    def sum_start(which, axis, value):
        sums[which, offsets[axis] + me[axis]] = value
        for k in range(counts[axis]):

            @pl.when(me[axis] != k)
            def _(k=k):
                sum_copy(which, axis, me[axis], k).start()

    def sum_end(which, axis):
        for k in range(counts[axis]):

            @pl.when(me[axis] != k)
            def _(k=k):
                sum_copy(which, axis, k, k).wait_recv()

        total = sums[which, offsets[axis]]
        for k in range(1, counts[axis]):
            total = total + sums[which, offsets[axis] + k]
        return total

    def padded(square):
        return jnp.concatenate([square, jnp.zeros((vecs, nz - vecs), F32)], axis=1)

    gram = None
    for s in range(ITERS):
        last = s == ITERS - 1
        for c in range(parts_c):
            ready(s, c)

            def step(k, _, s=s, c=c, last=last):
                x, y, i = place(k)
                totals = image(s, c, k)
                for t in range(GROUP):
                    field[s + 1, c, x + 1, y + t + 1] = totals[t]
                if last:
                    for t in range(GROUP):
                        parts[c, i + t] = split(totals[t])
                return 0

            lax.fori_loop(0, nodes // GROUP, step, 0)
            send(s + 1, c)
            if last:
                more = product(c, None)
                gram = more if gram is None else gram + more

    sum_start(0, 0, padded(fold(gram, vecs)))

    cross = None
    value = None
    for c in range(parts_c):
        ready(ITERS, c)

        def twice(y, _, c=c):
            low = field[ITERS, c, 0, y + 1]
            high = field[ITERS, c, nx + 1, half + y + 1]
            field[ITERS, c, 0, y + 1] = low + low
            field[ITERS, c, nx + 1, half + y + 1] = high + high
            return 0

        lax.fori_loop(0, half, twice, 0)

        def last_step(k, _, c=c):
            totals = image(ITERS, c, k)
            for t in range(GROUP):
                image_parts[k * GROUP + t] = split(totals[t])
            return 0

        lax.fori_loop(0, nodes // GROUP, last_step, 0)
        more = product(c, image_parts)
        cross = more if cross is None else cross + more
        value = sum_end(0, c)
        if c < 2:
            sum_start(0, c + 1, value)

    sum_start(1, 0, padded(fold(cross, vecs)))
    mixing = inverse_factor(value[:, :vecs] / total_rows, vecs)
    pieces = split(mixing)
    high, middle, low = (pieces[k * vecs : (k + 1) * vecs] for k in range(PIECES))
    none = jnp.zeros((vecs, vecs), BF16)
    mixer = jnp.concatenate(
        [
            jnp.concatenate([high, high, high], axis=1),
            jnp.concatenate([middle, middle, none], axis=1),
            jnp.concatenate([low, none, none], axis=1),
        ],
        axis=0,
    )

    for c in range(parts_c):

        def mix(k, _, c=c):
            x, y, i = place(k)
            right = jnp.concatenate([parts[c, i + t] for t in range(GROUP)], axis=1)
            out = jnp.dot(mixer, right, preferred_element_type=F32)
            out = out[:vecs] + out[vecs : 2 * vecs] + out[2 * vecs :]
            for t in range(GROUP):
                stage[c, x, y + t] = out[:, t * nz : (t + 1) * nz]
            return 0

        lax.fori_loop(0, nodes // GROUP, mix, 0)

        def put(k, _, c=c):
            x, y, _i = place(k)
            for t in range(GROUP):
                pltpu.make_async_copy(
                    stage.at[c, x, y + t], basis.at[c, :, x, y + t], local_sem.at[c]
                ).start()
            return 0

        lax.fori_loop(0, nodes // GROUP, put, 0)
        value = sum_end(1, c)
        if c < 2:
            sum_start(1, c + 1, value)

    form = value[:, :vecs]
    form = 0.5 * (form + form.T)
    first = exact_dot(mixing, form)
    coarse[...] = (
        lax.dot_general(
            first,
            mixing,
            (((1,), (1,)), ((), ())),
            precision=lax.Precision.HIGHEST,
            preferred_element_type=F32,
        )
        / total_rows
    )

    for s in range(ITERS + 1):
        for c in range(parts_c):
            each_side(lambda side: send_copy(s, c, side).wait_send())
    each_side(lambda side: phase_copy(side, side ^ 1).wait_send())
    for which in range(2):
        for axis in range(3):
            for k in range(counts[axis]):

                @pl.when(me[axis] != k)
                def _(which=which, axis=axis, k=k):
                    sum_copy(which, axis, me[axis], k).wait_send()

    for c in range(parts_c):
        pltpu.make_async_copy(
            stage.at[c], field.at[(0, c) + inner], local_sem.at[c]
        ).wait()


def on_device(counts, phase, lame, start):
    comps, vecs, nx, ny, nz = dims = start.shape
    nodes = nx * ny
    assert comps == 3 and 2 * nodes <= nz and ny % GROUP == 0
    slots = sum(counts)
    steps = ITERS + 1
    basis, coarse = pl.pallas_call(
        functools.partial(kernel, counts, dims),
        out_shape=(
            jax.ShapeDtypeStruct(start.shape, F32),
            jax.ShapeDtypeStruct((vecs, vecs), F32),
        ),
        in_specs=[
            pl.BlockSpec(memory_space=pltpu.HBM),
            pl.BlockSpec(memory_space=pltpu.HBM),
            pl.BlockSpec(memory_space=pltpu.HBM),
        ],
        out_specs=(
            pl.BlockSpec(memory_space=pltpu.HBM),
            pl.BlockSpec(memory_space=pltpu.VMEM),
        ),
        scratch_shapes=[
            pltpu.SMEM(lame.shape, F32),
            pltpu.VMEM(phase.shape, jnp.int32),
            pltpu.VMEM((steps, comps, nx + 2, ny + 2, vecs, nz), F32),
            pltpu.VMEM((comps, nx, ny, vecs, nz), F32),
            pltpu.VMEM((steps, comps, vecs, nz), F32),
            pltpu.VMEM((steps, comps, 2, vecs, nz), F32),
            pltpu.VMEM((vecs, nz), F32),
            pltpu.VMEM((phase.shape[0], ny, nz), F32),
            pltpu.VMEM((6, phase.shape[0], ny, nz), F32),
            pltpu.VMEM((12, nodes, nz), F32),
            pltpu.VMEM((comps, nodes, PIECES * vecs, nz), BF16),
            pltpu.VMEM((nodes, PIECES * vecs, nz), BF16),
            pltpu.VMEM((2, slots, vecs, nz), F32),
            pltpu.SemaphoreType.DMA((comps + 2,)),
            pltpu.SemaphoreType.DMA((6,)),
            pltpu.SemaphoreType.DMA((6,)),
            pltpu.SemaphoreType.DMA((steps, comps, 6)),
            pltpu.SemaphoreType.DMA((steps, comps, 6)),
            pltpu.SemaphoreType.DMA((2, slots)),
            pltpu.SemaphoreType.DMA((2, slots)),
        ],
        compiler_params=pltpu.CompilerParams(
            collective_id=0, has_side_effects=True, vmem_limit_bytes=67043328
        ),
    )(lame, phase, start)
    return basis, coarse


def solution(mesh):
    counts = tuple(mesh.shape[axis] for axis in AXES)
    spread = P(None, None, *AXES)
    return jax.shard_map(
        functools.partial(on_device, counts),
        mesh=mesh,
        in_specs=(P(*AXES), P(), spread),
        out_specs=(spread, P()),
        check_vma=False,
    )
```

```python
import functools

import jax
import jax.numpy as jnp
from jax import lax
from jax.experimental import pallas as pl
from jax.experimental.pallas import tpu as pltpu
from jax.sharding import PartitionSpec as P

ITERS = 3
PHASES = 2
BRICK = 4
PIECES = 3
GROUP = 4
AXES = ("gx", "gy", "gz")
MESH = pl.DeviceIdType.MESH
F32 = jnp.float32
BF16 = jnp.bfloat16


def split(value):
    pieces = []
    for _ in range(PIECES):
        piece = value.astype(BF16)
        pieces.append(piece)
        value = value - piece.astype(F32)
    return jnp.concatenate(pieces, axis=0)


def contract_last(left, right):
    return lax.dot_general(
        left, right, (((1,), (1,)), ((), ())), preferred_element_type=F32
    )


def exact_dot(left, right):
    return jnp.dot(
        left, right, precision=lax.Precision.HIGHEST, preferred_element_type=F32
    )


def fold(blocks, size):
    rows = blocks[:size]
    for k in range(1, PIECES):
        rows = rows + blocks[k * size : (k + 1) * size]
    total = rows[:, :size]
    for k in range(1, PIECES):
        total = total + rows[:, k * size : (k + 1) * size]
    return total


def inverse_factor(gram, size):
    row = lax.broadcasted_iota(jnp.int32, (size, size), 0)
    col = lax.broadcasted_iota(jnp.int32, (size, size), 1)
    both = jnp.concatenate([gram, jnp.where(row == col, 1.0, 0.0).astype(F32)], axis=1)
    rows = lax.broadcasted_iota(jnp.int32, both.shape, 0)
    for j in range(size):
        scale = lax.rsqrt(both[j : j + 1, j : j + 1])
        pivot = both[j : j + 1, :] * scale
        column = both[:, j : j + 1] * scale
        both = jnp.where(
            rows > j, both - column * pivot, jnp.where(rows == j, pivot, both)
        )
    return both[:, size:]


def kernel(
    counts,
    dims,
    lame_in,
    phase_hbm,
    start,
    basis,
    coarse,
    lame,
    phase,
    field,
    stage,
    edge_out,
    edge_in,
    edge_now,
    phase_own,
    phase_in,
    weights,
    parts,
    image_parts,
    sums,
    local_sem,
    phase_send,
    phase_recv,
    send_sem,
    recv_sem,
    sum_send,
    sum_recv,
):
    parts_c, vecs, nx, ny, nz = dims
    nodes = nx * ny
    total_rows = 1.0 * parts_c * nodes * nz * counts[0] * counts[1] * counts[2]
    me = [lax.axis_index(axis) for axis in AXES]
    half = ny // 2

    small = [
        pltpu.make_async_copy(phase_hbm, phase, local_sem.at[parts_c]),
        pltpu.make_async_copy(lame_in, lame, local_sem.at[parts_c + 1]),
    ]
    for copy in small:
        copy.start()

    def place(k):
        each = ny // GROUP
        return lax.div(k, each), lax.rem(k, each) * GROUP, k * GROUP

    for c in range(parts_c):

        def fetch(k, _, c=c):
            x, y, _i = place(k)
            for t in range(GROUP):
                pltpu.make_async_copy(
                    start.at[c, :, x, y + t],
                    field.at[0, c, x + 1, y + t + 1],
                    local_sem.at[c],
                ).start()
            return 0

        lax.fori_loop(0, nodes // GROUP, fetch, 0)

    inner = (pl.ds(1, nx), pl.ds(1, ny))

    def has(side):
        axis = side // 2
        return me[axis] > 0 if side % 2 == 0 else me[axis] < counts[axis] - 1

    def lacks(side):
        axis = side // 2
        return me[axis] == 0 if side % 2 == 0 else me[axis] == counts[axis] - 1

    def beside(side):
        axis = side // 2
        return {AXES[axis]: me[axis] - 1 if side % 2 == 0 else me[axis] + 1}

    plane = jnp.zeros((vecs, nz), F32)
    for side in range(2):
        at = 0 if side == 0 else nx + 1

        @pl.when(lacks(side))
        def _(at=at):
            def clear(i, _):
                for s in range(ITERS + 1):
                    for c in range(parts_c):
                        field[s, c, at, i + 1] = plane
                return 0

            lax.fori_loop(0, ny, clear, 0)

    for side in range(2, 4):
        at = 0 if side == 2 else ny + 1

        @pl.when(lacks(side))
        def _(at=at):
            def clear(i, _):
                for s in range(ITERS + 1):
                    for c in range(parts_c):
                        field[s, c, i + 1, at] = plane
                return 0

            lax.fori_loop(0, nx, clear, 0)

    def clear_half(i, _):
        for c in range(parts_c):
            field[ITERS, c, 0, half + i + 1] = plane
            field[ITERS, c, nx + 1, i + 1] = plane
        return 0

    lax.fori_loop(0, half, clear_half, 0)
    edge_in[...] = jnp.zeros(edge_in.shape, F32)
    phase_in[...] = jnp.zeros(phase_in.shape, F32)

    groups = (
        [{"gy": y, "gz": z} for y in range(counts[1]) for z in range(counts[2])],
        [{"gx": x} for x in range(counts[0])],
    )
    places = (me[1] * counts[2] + me[2], me[0])
    offsets = (0, len(groups[0]))
    barrier = pltpu.get_barrier_semaphore()
    for own_at, members in zip(places, groups):
        for k, member in enumerate(members):

            @pl.when(own_at != k)
            def _(member=member):
                pl.semaphore_signal(
                    barrier, inc=1, device_id=member, device_id_type=MESH
                )

    for copy in small:
        copy.wait()
    bricks_x, bricks_y, bricks_z = phase.shape
    spread = jnp.where(
        lax.broadcasted_iota(jnp.int32, (bricks_z, nz), 1) // BRICK
        == lax.broadcasted_iota(jnp.int32, (bricks_z, nz), 0),
        1.0,
        0.0,
    ).astype(F32)
    row_brick = lax.broadcasted_iota(jnp.int32, (ny, bricks_z), 0) // BRICK
    for bx in range(bricks_x):
        own = phase[bx].astype(F32)
        rows = jnp.zeros((ny, bricks_z), F32)
        for by in range(bricks_y):
            rows = jnp.where(
                row_brick == by,
                jnp.broadcast_to(own[by : by + 1], (ny, bricks_z)),
                rows,
            )
        phase_own[bx] = jnp.dot(rows, spread, preferred_element_type=F32)

    def face(s, c, side):
        if side == 0:
            src, dst = field.at[s, c, 1], field.at[s, c, nx + 1]
        elif side == 1:
            src, dst = field.at[s, c, nx], field.at[s, c, 0]
        elif side == 2:
            src = field.at[s, c, pl.ds(1, nx), 1]
            dst = field.at[s, c, pl.ds(1, nx), ny + 1]
        elif side == 3:
            src = field.at[s, c, pl.ds(1, nx), ny]
            dst = field.at[s, c, pl.ds(1, nx), 0]
        else:
            src, dst = edge_out.at[s, c], edge_in.at[s, c, 1 - side % 2]
        if side < 2:
            if s < ITERS:
                rows = pl.ds(1, ny)
            elif side == 0:
                rows = pl.ds(half + 1, ny - half)
            else:
                rows = pl.ds(1, half)
            src, dst = src.at[rows], dst.at[rows]
        return src, dst

    def send_copy(s, c, side):
        src, dst = face(s, c, side)
        return pltpu.make_async_remote_copy(
            src_ref=src,
            dst_ref=dst,
            send_sem=send_sem.at[s, c, side],
            recv_sem=recv_sem.at[s, c, side ^ 1],
            device_id=beside(side),
            device_id_type=MESH,
        )

    def recv_copy(s, c, side):
        src, dst = face(s, c, side ^ 1)
        return pltpu.make_async_remote_copy(
            src_ref=src,
            dst_ref=dst,
            send_sem=send_sem.at[s, c, side],
            recv_sem=recv_sem.at[s, c, side],
            device_id=beside(side),
            device_id_type=MESH,
        )

    lane = lax.broadcasted_iota(jnp.int32, (vecs, nz), 1)
    pair = lax.rem(lax.div(lane + 1, 2), nz // 2)

    def each_side(action, sides=range(6)):
        for side in sides:

            @pl.when(has(side))
            def _(side=side):
                action(side)

    def send(s, c):
        each_side(lambda side: send_copy(s, c, side).start(), range(4))
        edges = jnp.zeros((vecs, nz), F32)
        for i in range(nodes):
            value = field[s, c, i // ny + 1, i % ny + 1]
            edges = jnp.where(
                pair == i, pltpu.roll(value, 2 * i, 1) if i else value, edges
            )
        edge_out[s, c] = edges
        each_side(lambda side: send_copy(s, c, side).start(), range(4, 6))

    def receive(s, c):
        each_side(lambda side: recv_copy(s, c, side).wait_recv())

    def phase_copy(side, signal):
        return pltpu.make_async_remote_copy(
            src_ref=phase_own,
            dst_ref=phase_in.at[signal],
            send_sem=phase_send.at[side],
            recv_sem=phase_recv.at[signal],
            device_id=beside(side),
            device_id_type=MESH,
        )

    for c in range(parts_c):
        pltpu.make_async_copy(
            field.at[(1, c) + inner], field.at[(0, c) + inner], local_sem.at[c]
        ).wait()
        if c == 0:
            pl.semaphore_wait(barrier, len(groups[0]) + len(groups[1]) - 2)
            each_side(lambda side: phase_copy(side, side ^ 1).start())
        send(0, c)

    each_side(lambda side: phase_copy(side, side).wait_recv())
    line = lax.broadcasted_iota(jnp.int32, (ny, nz), 0)
    across = lax.broadcasted_iota(jnp.int32, (ny, nz), 1)

    def material(kinds):
        shear = jnp.zeros(kinds.shape, F32)
        first = jnp.zeros(kinds.shape, F32)
        for index in range(PHASES):
            hit = kinds == float(index)
            shear = shear + jnp.where(hit, lame[index, 0], 0.0)
            first = first + jnp.where(hit, lame[index, 1], 0.0)
        return shear, first + shear

    for x in range(nx):
        bx = x // BRICK
        own = phase_own[bx]
        others = [
            phase_own[(x - 1) // BRICK] if x > 0 else phase_in[0, bricks_x - 1],
            phase_own[(x + 1) // BRICK] if x < nx - 1 else phase_in[1, 0],
            pltpu.roll(jnp.where(line == ny - 1, phase_in[2, bx], own), 1, 0),
            pltpu.roll(jnp.where(line == 0, phase_in[3, bx], own), ny - 1, 0),
            pltpu.roll(jnp.where(across == nz - 1, phase_in[4, bx], own), 1, 1),
            pltpu.roll(jnp.where(across == 0, phase_in[5, bx], own), nz - 1, 1),
        ]
        shear_c, grow_c = material(own)
        for side in range(6):
            shear_n, grow_n = material(others[side])
            w_shear = 0.5 * (shear_c + shear_n)
            w_grow = 0.5 * (grow_c + grow_n)
            weights[2 * side, pl.ds(x * ny, ny), :] = w_shear
            weights[2 * side + 1, pl.ds(x * ny, ny), :] = w_shear + w_grow

    def image(s, c, k):
        x, y, i = place(k)
        column = [field[s, c, x + 1, y + t] for t in range(GROUP + 2)]
        edges = edge_now[...]
        totals = []
        for t in range(GROUP):
            centre = column[t + 1]
            border = pltpu.roll(edges, nz - 2 * t - 2 * i, 1)
            others = [
                field[s, c, x, y + t + 1],
                field[s, c, x + 2, y + t + 1],
                column[t],
                column[t + 2],
                jnp.where(lane == 0, border, pltpu.roll(centre, 1, 1)),
                jnp.where(lane == nz - 1, border, pltpu.roll(centre, nz - 1, 1)),
            ]
            total = None
            for side in range(6):
                which = 2 * side + (1 if side // 2 == c else 0)
                weight = weights[which, pl.ds(i + t, 1), :]
                term = weight * (centre - others[side])
                total = term if total is None else total + term
            totals.append(total)
        return totals

    def ready(s, c):
        receive(s, c)
        edge_now[...] = jnp.where(
            lax.rem(lane, 2) == 0,
            pltpu.roll(edge_in[s, c, 0], 1, 1),
            pltpu.roll(edge_in[s, c, 1], nz - 1, 1),
        )

    def product(c, other):
        total = None
        for x in range(nx):
            left = jnp.concatenate(
                [parts[c, x * ny + y] for y in range(ny)], axis=1
            )
            right = (
                left
                if other is None
                else jnp.concatenate([other[x * ny + y] for y in range(ny)], axis=1)
            )
            more = contract_last(left, right)
            total = more if total is None else total + more
        return total

    def sum_copy(which, stage_at, slot, other):
        at = offsets[stage_at] + slot
        return pltpu.make_async_remote_copy(
            src_ref=sums.at[which, at],
            dst_ref=sums.at[which, at],
            send_sem=sum_send.at[which, offsets[stage_at] + other],
            recv_sem=sum_recv.at[which, at],
            device_id=groups[stage_at][other],
            device_id_type=MESH,
        )

    def each_member(stage_at, action):
        for k in range(len(groups[stage_at])):

            @pl.when(places[stage_at] != k)
            def _(k=k):
                action(k)

    def sum_start(which, stage_at, value):
        mine = places[stage_at]
        sums[which, offsets[stage_at] + mine] = value
        each_member(stage_at, lambda k: sum_copy(which, stage_at, mine, k).start())

    def sum_end(which, stage_at):
        each_member(stage_at, lambda k: sum_copy(which, stage_at, k, k).wait_recv())
        total = sums[which, offsets[stage_at]]
        for k in range(1, len(groups[stage_at])):
            total = total + sums[which, offsets[stage_at] + k]
        return total

    across_n = nz // vecs
    down_n = vecs // across_n

    def packed(square):
        pieces = [square[k * down_n : (k + 1) * down_n] for k in range(across_n)]
        return jnp.concatenate(pieces, axis=1)

    def unpacked(value):
        pieces = [value[:, k * vecs : (k + 1) * vecs] for k in range(across_n)]
        return jnp.concatenate(pieces, axis=0)

    gram = None
    for s in range(ITERS):
        last = s == ITERS - 1
        for c in range(parts_c):
            ready(s, c)

            def step(k, _, s=s, c=c, last=last):
                x, y, i = place(k)
                totals = image(s, c, k)
                for t in range(GROUP):
                    field[s + 1, c, x + 1, y + t + 1] = totals[t]
                if last:
                    for t in range(GROUP):
                        parts[c, i + t] = split(totals[t])
                return 0

            lax.fori_loop(0, nodes // GROUP, step, 0)
            send(s + 1, c)
            if last:
                more = product(c, None)
                gram = more if gram is None else gram + more

    sum_start(0, 0, packed(fold(gram, vecs)))

    cross = None
    for c in range(parts_c):
        ready(ITERS, c)

        def twice(y, _, c=c):
            low = field[ITERS, c, 0, y + 1]
            high = field[ITERS, c, nx + 1, half + y + 1]
            field[ITERS, c, 0, y + 1] = low + low
            field[ITERS, c, nx + 1, half + y + 1] = high + high
            return 0

        lax.fori_loop(0, half, twice, 0)

        def last_step(k, _, c=c):
            totals = image(ITERS, c, k)
            for t in range(GROUP):
                image_parts[k * GROUP + t] = split(totals[t])
            return 0

        lax.fori_loop(0, nodes // GROUP, last_step, 0)
        more = product(c, image_parts)
        cross = more if cross is None else cross + more
        if c == 0:
            sum_start(0, 1, sum_end(0, 0))

    sum_start(1, 0, packed(fold(cross, vecs)))
    mixing = inverse_factor(unpacked(sum_end(0, 1)) / total_rows, vecs)
    sum_start(1, 1, sum_end(1, 0))
    pieces = split(mixing)
    high, middle, low = (pieces[k * vecs : (k + 1) * vecs] for k in range(PIECES))
    none = jnp.zeros((vecs, vecs), BF16)
    mixer = jnp.concatenate(
        [
            jnp.concatenate([high, high, high], axis=1),
            jnp.concatenate([middle, middle, none], axis=1),
            jnp.concatenate([low, none, none], axis=1),
        ],
        axis=0,
    )

    for c in range(parts_c):

        def mix(k, _, c=c):
            x, y, i = place(k)
            right = jnp.concatenate([parts[c, i + t] for t in range(GROUP)], axis=1)
            out = jnp.dot(mixer, right, preferred_element_type=F32)
            out = out[:vecs] + out[vecs : 2 * vecs] + out[2 * vecs :]
            for t in range(GROUP):
                stage[c, x, y + t] = out[:, t * nz : (t + 1) * nz]
            return 0

        lax.fori_loop(0, nodes // GROUP, mix, 0)

        def put(k, _, c=c):
            x, y, _i = place(k)
            for t in range(GROUP):
                pltpu.make_async_copy(
                    stage.at[c, x, y + t], basis.at[c, :, x, y + t], local_sem.at[c]
                ).start()
            return 0

        lax.fori_loop(0, nodes // GROUP, put, 0)
    form = unpacked(sum_end(1, 1))
    form = 0.5 * (form + form.T)
    first = exact_dot(mixing, form)
    coarse[...] = (
        lax.dot_general(
            first,
            mixing,
            (((1,), (1,)), ((), ())),
            precision=lax.Precision.HIGHEST,
            preferred_element_type=F32,
        )
        / total_rows
    )

    for s in range(ITERS + 1):
        for c in range(parts_c):
            each_side(lambda side: send_copy(s, c, side).wait_send())
    each_side(lambda side: phase_copy(side, side ^ 1).wait_send())
    for which in range(2):
        for stage_at in range(2):
            each_member(
                stage_at,
                lambda k: sum_copy(which, stage_at, places[stage_at], k).wait_send(),
            )

    for c in range(parts_c):
        pltpu.make_async_copy(
            stage.at[c], field.at[(0, c) + inner], local_sem.at[c]
        ).wait()


def on_device(counts, phase, lame, start):
    comps, vecs, nx, ny, nz = dims = start.shape
    nodes = nx * ny
    assert nz % vecs == 0 and vecs % (nz // vecs) == 0
    assert comps == 3 and 2 * nodes <= nz and ny % GROUP == 0
    slots = counts[0] + counts[1] * counts[2]
    steps = ITERS + 1
    basis, coarse = pl.pallas_call(
        functools.partial(kernel, counts, dims),
        out_shape=(
            jax.ShapeDtypeStruct(start.shape, F32),
            jax.ShapeDtypeStruct((vecs, vecs), F32),
        ),
        in_specs=[
            pl.BlockSpec(memory_space=pltpu.HBM),
            pl.BlockSpec(memory_space=pltpu.HBM),
            pl.BlockSpec(memory_space=pltpu.HBM),
        ],
        out_specs=(
            pl.BlockSpec(memory_space=pltpu.HBM),
            pl.BlockSpec(memory_space=pltpu.VMEM),
        ),
        scratch_shapes=[
            pltpu.SMEM(lame.shape, F32),
            pltpu.VMEM(phase.shape, jnp.int32),
            pltpu.VMEM((steps, comps, nx + 2, ny + 2, vecs, nz), F32),
            pltpu.VMEM((comps, nx, ny, vecs, nz), F32),
            pltpu.VMEM((steps, comps, vecs, nz), F32),
            pltpu.VMEM((steps, comps, 2, vecs, nz), F32),
            pltpu.VMEM((vecs, nz), F32),
            pltpu.VMEM((phase.shape[0], ny, nz), F32),
            pltpu.VMEM((6, phase.shape[0], ny, nz), F32),
            pltpu.VMEM((12, nodes, nz), F32),
            pltpu.VMEM((comps, nodes, PIECES * vecs, nz), BF16),
            pltpu.VMEM((nodes, PIECES * vecs, nz), BF16),
            pltpu.VMEM((2, slots, vecs * vecs // nz, nz), F32),
            pltpu.SemaphoreType.DMA((comps + 2,)),
            pltpu.SemaphoreType.DMA((6,)),
            pltpu.SemaphoreType.DMA((6,)),
            pltpu.SemaphoreType.DMA((steps, comps, 6)),
            pltpu.SemaphoreType.DMA((steps, comps, 6)),
            pltpu.SemaphoreType.DMA((2, slots)),
            pltpu.SemaphoreType.DMA((2, slots)),
        ],
        compiler_params=pltpu.CompilerParams(
            collective_id=0, has_side_effects=True, vmem_limit_bytes=67043328
        ),
    )(lame, phase, start)
    return basis, coarse


def solution(mesh):
    counts = tuple(mesh.shape[axis] for axis in AXES)
    spread = P(None, None, *AXES)
    return jax.shard_map(
        functools.partial(on_device, counts),
        mesh=mesh,
        in_specs=(P(*AXES), P(), spread),
        out_specs=(spread, P()),
        check_vma=False,
    )
```
